256 devices in a mesh: sec: 4 (over x), feat: 16 (over z, core), row: 4 (over y).
Axes of the slice: x: 4, y: 4, z: 8, core: 2. Of those that a mesh axis runs over, the one named last changes fastest.
Arguments:
- inputs: bfloat16 [4, 1024, 2304], P('sec', 'row', 'feat'), may hold values from -6 to 6
- enc_weight: bfloat16 [4, 2304, 16384], P('sec', None, 'feat'), may hold values from -0.125 to 0.125
- enc_bias: float32 [4, 16384], P('sec', 'feat'), may hold values from -0.5 to 0.5
- dec_weight: bfloat16 [4, 4, 16384, 2304], P('sec', None, 'feat', 'row'), may hold values from -0.046875 to 0.046875
- dec_bias: float32 [4, 2304], P('sec', 'row'), may hold values from -3 to 3
Outputs:
- recon: bfloat16 [4, 1024, 2304], P('sec', 'feat', 'row')
The draws below stay inside these ranges and needn't reach their ends.
All inputs are finite; a program needn't handle non-finite values.
Results may differ from the reference program's by a relative error of at most 0.0047.
Values may be sent and summed in bfloat16 or wider, within the bound.
No kernel may reach another device: no remote copies, remote signals or barrier semaphores. Data moves between devices by JAX's collectives and lax.ppermute only.
A program may use at most 64 MiB of HBM per device.

```python
import jax
import jax.numpy as jnp

D = 2304
F = 16384
S = 4
TOKENS = 1024


def level_of(own_key, shape, pieces, low, largest):
    gain = 1.0
    for dim, shards_of in pieces:
        steps = jax.random.uniform(jax.random.fold_in(jax.random.fold_in(own_key, 6), dim), (shards_of,), jnp.float32, low / len(pieces), largest / len(pieces))
        gain = gain * jnp.repeat(jnp.exp(steps), shape[dim] // shards_of).reshape((-1,) + (1,) * (len(shape) - 1 - dim))
    return gain


def gaussian(stream_key, dims, deviation, most, shards=(), dtype=jnp.bfloat16):
    result = jax.random.normal(stream_key, dims, jnp.float32) * deviation
    if len(shards) > 0:
        result = level_of(stream_key, dims, shards, -0.22, 0.18) * result
    return jnp.clip(result, min=-most, max=most).astype(dtype)


def setup_inputs(seed: int = 0) -> dict:
    seeds = jax.random.split(jax.random.key(seed), 6)
    inputs = gaussian(seeds[0], (S, TOKENS, D), 1.0, 6.0, ((0, 4), (1, 4), (2, 16)))
    enc_weight = gaussian(seeds[1], (S, D, F), D ** -0.5, 0.125, ((0, 4), (2, 16)))
    enc_bias = jnp.clip(jax.random.uniform(seeds[2], (S, F), jnp.float32, -0.5, 0.5) * level_of(seeds[2], (S, F), ((0, 4), (1, 16)), -0.4, 0.0), -0.5, 0.5)
    dec_weight = gaussian(seeds[3], (S, S, F, D), F ** -0.5, 0.046875, ((0, 4), (2, 16), (3, 4)))
    dec_bias = gaussian(seeds[4], (S, D), 0.5, 3.0, ((0, 4), (1, 4)), jnp.float32)
    return dict(inputs=inputs, enc_weight=enc_weight, enc_bias=enc_bias, dec_weight=dec_weight, dec_bias=dec_bias)


def reference(inputs, enc_weight, enc_bias, dec_weight, dec_bias):
    features = []
    for source in range(S):
        hidden = jnp.dot(inputs[source], enc_weight[source], preferred_element_type=jnp.float32) + enc_bias[source]
        features.append(jnp.maximum(hidden, 0.0).astype(jnp.bfloat16))
    results = []
    for target in range(S):
        totals = jnp.zeros((TOKENS, D), jnp.float32)
        for source in range(target + 1):
            totals = totals + jnp.dot(features[source], dec_weight[target, source], preferred_element_type=jnp.float32)
        results.append((totals + dec_bias[target]).astype(jnp.bfloat16))
    return jnp.stack(results)
```

```python
import jax
import jax.numpy as jnp
from jax import lax
from jax.sharding import PartitionSpec as P


CHIPS = 8
ROWS = 4


def ring(shift):
    return [(i, (i + shift) % ROWS) for i in range(ROWS)]


def hop(shift):
    return [(i, ((i // 2 + shift) % CHIPS) * 2 + i % 2) for i in range(2 * CHIPS)]


SWAP = [(i, i ^ 1) for i in range(2 * CHIPS)]
BOTH = [(i, ((i // 2 + (1 if i % 2 == 0 else -1)) % CHIPS) * 2 + i % 2) for i in range(2 * CHIPS)]


def gather_inputs(own, core, chip):
    other = lax.ppermute(own, "feat", SWAP)
    block = jnp.where(core == 0, jnp.concatenate([own, other]), jnp.concatenate([other, own]))
    b1 = lax.ppermute(block, "feat", BOTH)
    b2 = lax.ppermute(b1, "feat", BOTH)
    b3 = lax.ppermute(b2, "feat", BOTH)
    b4 = lax.ppermute(b3, "feat", BOTH)
    s1, s2, s3 = jnp.split(lax.ppermute(jnp.concatenate([b1, b2, b3]), "feat", SWAP), 3)
    sign = 1 - 2 * core
    size = block.shape[0]
    whole = jnp.zeros((CHIPS * size, own.shape[1]), own.dtype)
    for piece, shift in ((block, 0), (b1, -1), (b2, -2), (b3, -3), (b4, -4), (s1, 1), (s2, 2), (s3, 3)):
        at = (chip + sign * shift) & (CHIPS - 1)
        whole = lax.dynamic_update_slice(whole, piece, (at * size, 0))
    return whole


def gather_rows(own):
    half = own.shape[0] // 2
    before = lax.ppermute(own, "row", ring(1))
    after = lax.ppermute(own, "row", ring(-1))
    first = lax.ppermute(before[:half], "row", ring(1))
    second = lax.ppermute(after[half:], "row", ring(-1))
    return jnp.concatenate([own, after, first, second, before])


def scatter_sum(partial, core, chip, row):
    width = partial.shape[1]
    pieces = partial.reshape(ROWS, 2, 2, 64, width)
    mine = jnp.where(core == 0, pieces[:, :, 0], pieces[:, :, 1])
    theirs = jnp.where(core == 0, pieces[:, :, 1], pieces[:, :, 0]).astype(jnp.bfloat16)
    mine = mine + lax.ppermute(theirs, "feat", SWAP).astype(jnp.float32)
    mine = mine.reshape(CHIPS, 64, width)
    send = mine.astype(jnp.bfloat16)

    def of(array, shift):
        to = chip + shift
        at = (to - 2 * row) & (CHIPS - 1)
        return lax.dynamic_index_in_dim(array, at, 0, keepdims=False)

    got = [lax.ppermute(of(send, d), "feat", hop(d)) for d in (4, 3, 5, 2, 6, 1, 7)]
    total = of(mine, 0)
    for g in got:
        total = total + g.astype(jnp.float32)
    return total


def per_device(inputs, enc_weight, enc_bias, dec_weight, dec_bias):
    encoder = enc_weight[0]
    decoders = dec_weight[0]
    sec = lax.axis_index("sec")
    feat = lax.axis_index("feat")
    row = lax.axis_index("row")
    core, chip = feat & 1, feat >> 1

    lent = jnp.where(sec == 3, 0, 1)
    foreign_a = lax.ppermute(lax.dynamic_index_in_dim(decoders, lent, 0, keepdims=False), "sec", [(3, 0), (2, 1)])
    foreign_b = lax.ppermute(decoders[2], "sec", [(3, 2)])
    foreign = foreign_a + foreign_b

    whole = gather_inputs(inputs[0].T, core, chip)
    hidden = lax.dot_general(whole, encoder, (((0,), (0,)), ((), ())), preferred_element_type=jnp.float32)
    features = jnp.maximum(hidden + enc_bias[0], 0.0).astype(jnp.bfloat16)

    import_b = lax.ppermute(features, "sec", [(0, 2), (1, 3)])
    import_a = lax.ppermute(features, "sec", [(0, 1)])
    every_own = gather_rows(features)
    every_import = gather_rows(import_a + import_b)

    def decode(block, weight):
        return jnp.dot(block, weight, preferred_element_type=jnp.float32)

    lent_sum = scatter_sum(decode(every_own, foreign), core, chip, row)
    from_a = lax.ppermute(lent_sum, "sec", [(0, 3), (1, 2)])
    from_b = lax.ppermute(lent_sum, "sec", [(2, 3)])

    own_weight = lax.dynamic_index_in_dim(decoders, sec, 0, keepdims=False)
    import_weight = lax.dynamic_index_in_dim(decoders, jnp.where(sec == 3, 1, 0), 0, keepdims=False)
    partial = decode(every_own, own_weight) + decode(every_import, import_weight)
    own_sum = scatter_sum(partial, core, chip, row)
    return (own_sum + from_a + from_b + dec_bias[0]).astype(jnp.bfloat16)[None]


def solution(mesh):
    in_specs = (
        P("sec", "row", "feat"),
        P("sec", None, "feat"),
        P("sec", "feat"),
        P("sec", None, "feat", "row"),
        P("sec", "row"),
    )
    out_specs = P("sec", "feat", "row")
    return jax.shard_map(
        per_device, mesh=mesh, in_specs=in_specs, out_specs=out_specs, check_vma=False
    )
```

```python
import jax
import jax.numpy as jnp
from jax import lax
from jax.experimental import pallas as pl
from jax.experimental.pallas import tpu as pltpu
from jax.sharding import PartitionSpec as P


CHIPS = 8
ROWS = 4
PIECE = 64
ANY = pl.BlockSpec(memory_space=pl.ANY)
SMEM = pl.BlockSpec(memory_space=pltpu.SMEM)


def ring(shift):
    return [(i, (i + shift) % ROWS) for i in range(ROWS)]


def hop(shift):
    return [(i, ((i // 2 + shift) % CHIPS) * 2 + i % 2) for i in range(2 * CHIPS)]


SWAP = [(i, i ^ 1) for i in range(2 * CHIPS)]
BOTH = [(i, ((i // 2 + (1 if i % 2 == 0 else -1)) % CHIPS) * 2 + i % 2) for i in range(2 * CHIPS)]


def gather_inputs(own, core, chip):
    other = lax.ppermute(own, "feat", SWAP)
    block = jnp.where(core == 0, jnp.concatenate([own, other]), jnp.concatenate([other, own]))
    b1 = lax.ppermute(block, "feat", BOTH)
    b2 = lax.ppermute(b1, "feat", BOTH)
    b3 = lax.ppermute(b2, "feat", BOTH)
    b4 = lax.ppermute(b3, "feat", BOTH)
    s1, s2, s3 = jnp.split(lax.ppermute(jnp.concatenate([b1, b2, b3]), "feat", SWAP), 3)
    sign = 1 - 2 * core
    size = block.shape[0]
    whole = jnp.zeros((CHIPS * size, own.shape[1]), own.dtype)
    for piece, shift in ((block, 0), (b1, -1), (b2, -2), (b3, -3), (b4, -4), (s1, 1), (s2, 2), (s3, 3)):
        at = (chip + sign * shift) & (CHIPS - 1)
        whole = lax.dynamic_update_slice(whole, piece, (at * size, 0))
    return whole


def encode_kernel(x_ref, weight_ref, bias_ref, out_ref, turned):
    @pl.when(pl.program_id(0) == 0)
    def _():
        turned[...] = x_ref[...].T

    hidden = jnp.dot(turned[...], weight_ref[...], preferred_element_type=jnp.float32)
    out_ref[...] = jnp.maximum(hidden + bias_ref[...], 0.0).astype(out_ref.dtype)


def encode(x, weight, bias):
    model, tokens = x.shape
    width = weight.shape[1]
    step = 256
    return pl.pallas_call(
        encode_kernel,
        grid=(width // step,),
        in_specs=[
            pl.BlockSpec((model, tokens), lambda i: (0, 0)),
            pl.BlockSpec((model, step), lambda i: (0, i)),
            pl.BlockSpec((1, step), lambda i: (0, i)),
        ],
        out_specs=pl.BlockSpec((tokens, step), lambda i: (0, i)),
        out_shape=jax.ShapeDtypeStruct((tokens, width), jnp.bfloat16),
        scratch_shapes=[pltpu.VMEM((tokens, model), x.dtype)],
        name="encode",
    )(x, weight, bias)


def gather_rows(own):
    half = own.shape[0] // 2
    before = lax.ppermute(own, "row", ring(1))
    after = lax.ppermute(own, "row", ring(-1))
    first = lax.ppermute(before[:half], "row", ring(1))
    second = lax.ppermute(after[half:], "row", ring(-1))
    return own, before, after, first, second


def decode(where, rows, weights, start, split):
    tokens, count = rows[0].shape
    half = tokens // 2
    width = weights[0].shape[1]
    n = len(weights)
    has_start = start is not None

    def kernel(where_ref, own, before, after, first, second, *rest):
        sources = rest[:n]
        rest = rest[n:]
        if has_start:
            start_ref, *rest = rest
        if split:
            mine_ref, theirs_ref, *rest = rest
        else:
            out_ref, *rest = rest
        block, weight, total, sem_in, sem_weight, sem_start, sem_out, *rest = rest
        core, chip, row = where_ref[0], where_ref[1], where_ref[2]
        parts = [
            [pltpu.make_async_copy(own, block.at[0], sem_in.at[0])],
            [pltpu.make_async_copy(after, block.at[1], sem_in.at[1])],
            [pltpu.make_async_copy(before, block.at[3], sem_in.at[3])],
            [
                pltpu.make_async_copy(first, block.at[2, :half], sem_in.at[2]),
                pltpu.make_async_copy(second, block.at[2, half:], sem_in.at[4]),
            ],
        ]
        for number, source in enumerate(sources):

            @pl.when(where_ref[4] == number)
            def _(source=source):
                pltpu.make_async_copy(source.at[where_ref[3]], weight, sem_weight.at[0]).start()

        for part in parts:
            for copy in part:
                copy.start()
        if has_start:
            starts = [pltpu.make_async_copy(start_ref.at[j], total.at[j], sem_start.at[j]) for j in (0, 1, 3, 2)]
            for copy in starts:
                copy.start()
        pltpu.make_async_copy(sources[0].at[0], weight, sem_weight.at[0]).wait()
        outs = []
        for number, j in enumerate((0, 1, 3, 2)):
            for copy in parts[number]:
                copy.wait()
            value = lax.dot_general(block[j], weight[...], (((1,), (1,)), ((), ())), preferred_element_type=jnp.float32)
            if has_start:
                starts[number].wait()
                value = value + total[j]
            if not split:
                total[j] = value
                copy = pltpu.make_async_copy(total.at[j], out_ref.at[j], sem_out.at[j])
                copy.start()
                outs.append(copy)
                continue
            mine, theirs = rest
            for h in range(2):
                at = (2 * ((row + j) & (ROWS - 1)) + h - (chip if split == "relative" else 0)) & (CHIPS - 1)
                low = value[2 * h * PIECE : (2 * h + 1) * PIECE]
                high = value[(2 * h + 1) * PIECE : (2 * h + 2) * PIECE]
                mine[at] = jnp.where(core == 0, low, high)
                theirs[at] = jnp.where(core == 0, high, low).astype(jnp.bfloat16)
                for k, (source, target) in enumerate(((theirs, theirs_ref), (mine, mine_ref))):
                    copy = pltpu.make_async_copy(source.at[at], target.at[at], sem_out.at[4 * number + 2 * h + k])
                    copy.start()
                    outs.append(copy)
        for copy in outs:
            copy.wait()

    scratch = [
        pltpu.VMEM((ROWS, tokens, count), jnp.bfloat16),
        pltpu.VMEM((width, count), jnp.bfloat16),
        pltpu.VMEM((ROWS, tokens, width), jnp.float32),
        pltpu.SemaphoreType.DMA((5,)),
        pltpu.SemaphoreType.DMA((1,)),
        pltpu.SemaphoreType.DMA((4,)),
        pltpu.SemaphoreType.DMA((16,)),
    ]
    if split:
        shape = (CHIPS, PIECE, width)
        scratch += [pltpu.VMEM(shape, jnp.float32), pltpu.VMEM(shape, jnp.bfloat16)]
        out_shape = (jax.ShapeDtypeStruct(shape, jnp.float32), jax.ShapeDtypeStruct(shape, jnp.bfloat16))
        out_specs = (ANY, ANY)
    else:
        out_shape = jax.ShapeDtypeStruct((ROWS, tokens, width), jnp.float32)
        out_specs = ANY
    operands = list(rows) + list(weights) + ([start] if has_start else [])
    return pl.pallas_call(
        kernel,
        in_specs=[SMEM] + [ANY] * len(operands),
        out_specs=out_specs,
        out_shape=out_shape,
        scratch_shapes=scratch,
    )(where, *operands)


def per_device(inputs, enc_weight, enc_bias, dec_weight, dec_bias):
    decoders = jnp.swapaxes(dec_weight[0], 1, 2)
    sec = lax.axis_index("sec")
    feat = lax.axis_index("feat")
    row = lax.axis_index("row")
    core, chip = feat & 1, feat >> 1

    def where(index, taken):
        return jnp.stack([jnp.asarray(v, jnp.int32) for v in (core, chip, row, index, taken)])

    lent = jnp.where(sec == 3, 0, 1)
    lent_a = lax.ppermute(lax.dynamic_slice_in_dim(decoders, lent, 1, 0), "sec", [(3, 0), (2, 1)])
    lent_b = lax.ppermute(decoders[2:3], "sec", [(3, 2)])

    whole = gather_inputs(inputs[0].T, core, chip)
    features = encode(whole, enc_weight[0], enc_bias)

    every_own = gather_rows(features)
    brought_b = lax.ppermute(features, "sec", [(0, 2), (1, 3)])
    brought_a = lax.ppermute(features, "sec", [(0, 1)])
    every_brought = gather_rows(brought_a + brought_b)

    mine, theirs = decode(where(0, jnp.where(sec == 2, 1, 0)), every_own, (lent_a, lent_b), None, "absolute")
    pair = mine + lax.ppermute(theirs, "feat", SWAP).astype(jnp.float32)
    same_core = [[2 * i + c for i in range(CHIPS)] for c in range(2)]
    spread = lax.all_to_all(pair.astype(jnp.bfloat16), "feat", 0, 0, tiled=True, axis_index_groups=same_core)
    lent_sum = jnp.sum(spread.astype(jnp.float32), axis=0)
    back_a = lax.ppermute(lent_sum, "sec", [(0, 3), (1, 2)])
    back_b = lax.ppermute(lent_sum, "sec", [(2, 3)])

    start = decode(where(sec, 0), every_own, (decoders,), None, "")
    mine, theirs = decode(where(jnp.where(sec == 3, 1, 0), 0), every_brought, (decoders,), start, "relative")
    pair = mine + lax.ppermute(theirs, "feat", SWAP).astype(jnp.float32)
    send = pair.astype(jnp.bfloat16)
    got = [lax.ppermute(send[d], "feat", hop(d)) for d in (4, 3, 5, 2, 6, 1, 7)]
    total = pair[0]
    for g in got:
        total = total + g.astype(jnp.float32)
    return (total + back_a + back_b + dec_bias[0]).astype(jnp.bfloat16)[None]


def solution(mesh):
    in_specs = (
        P("sec", "row", "feat"),
        P("sec", None, "feat"),
        P("sec", "feat"),
        P("sec", None, "feat", "row"),
        P("sec", "row"),
    )
    out_specs = P("sec", "feat", "row")

    return jax.shard_map(per_device, mesh=mesh, in_specs=in_specs, out_specs=out_specs, check_vma=False)
```

```python
import jax
import jax.numpy as jnp
from jax import lax
from jax.experimental import pallas as pl
from jax.experimental.pallas import tpu as pltpu
from jax.sharding import PartitionSpec as P


CHIPS = 8
ROWS = 4
PIECE = 64
VMEM = pl.BlockSpec(memory_space=pltpu.VMEM)
SMEM = pl.BlockSpec(memory_space=pltpu.SMEM)


def ring(shift):
    return [(i, (i + shift) % ROWS) for i in range(ROWS)]


def hop(shift):
    return [(i, ((i // 2 + shift) % CHIPS) * 2 + i % 2) for i in range(2 * CHIPS)]


SWAP = [(i, i ^ 1) for i in range(2 * CHIPS)]
BOTH = [(i, ((i // 2 + (1 if i % 2 == 0 else -1)) % CHIPS) * 2 + i % 2) for i in range(2 * CHIPS)]


def gather_inputs(own, core, chip):
    other = lax.ppermute(own, "feat", SWAP)
    block = jnp.where(core == 0, jnp.concatenate([own, other]), jnp.concatenate([other, own]))
    b1 = lax.ppermute(block, "feat", BOTH)
    b2 = lax.ppermute(b1, "feat", BOTH)
    b3 = lax.ppermute(b2, "feat", BOTH)
    b4 = lax.ppermute(b3, "feat", BOTH)
    s1, s2, s3 = jnp.split(lax.ppermute(jnp.concatenate([b1, b2, b3]), "feat", SWAP), 3)
    sign = 1 - 2 * core
    size = block.shape[0]
    whole = jnp.zeros((CHIPS * size, own.shape[1]), own.dtype)
    for piece, shift in ((block, 0), (b1, -1), (b2, -2), (b3, -3), (b4, -4), (s1, 1), (s2, 2), (s3, 3)):
        at = (chip + sign * shift) & (CHIPS - 1)
        whole = lax.dynamic_update_slice(whole, piece, (at * size, 0))
    return whole


def encode(x, weight, bias):
    hidden = lax.dot_general(x, weight, (((0,), (0,)), ((), ())), preferred_element_type=jnp.float32)
    return jnp.maximum(hidden + bias, 0.0).astype(jnp.bfloat16)


def gather_rows(own):
    half = own.shape[0] // 2
    before = lax.ppermute(own, "row", ring(1))
    after = lax.ppermute(own, "row", ring(-1))
    first = lax.ppermute(before[:half], "row", ring(1))
    second = lax.ppermute(after[half:], "row", ring(-1))
    return own, before, after, first, second


def decode(where, rows, weight, start, split):
    tokens, count = rows[0].shape
    width = weight.shape[0]
    has_start = start is not None

    def kernel(where_ref, own, before, after, first, second, weight_ref, *rest):
        core, chip, row = where_ref[0], where_ref[1], where_ref[2]
        if has_start:
            start_ref, *rest = rest
        if split:
            mine_ref, theirs_ref, turned = rest
        else:
            out_ref, turned = rest
        turned[...] = weight_ref[...].T
        for j, parts in enumerate(((own,), (after,), (first, second), (before,))):
            block = parts[0][...] if len(parts) == 1 else jnp.concatenate([p[...] for p in parts])
            value = jnp.dot(block, turned[...], preferred_element_type=jnp.float32)
            if has_start:
                value = value + start_ref[j]
            if not split:
                out_ref[j] = value
                continue
            for h in range(2):
                at = (2 * ((row + j) & (ROWS - 1)) + h - (chip if split == "relative" else 0)) & (CHIPS - 1)
                low = value[2 * h * PIECE : (2 * h + 1) * PIECE]
                high = value[(2 * h + 1) * PIECE : (2 * h + 2) * PIECE]
                mine_ref[at] = jnp.where(core == 0, low, high)
                theirs_ref[at] = jnp.where(core == 0, high, low).astype(jnp.bfloat16)

    if split:
        shape = (CHIPS, PIECE, width)
        out_shape = (jax.ShapeDtypeStruct(shape, jnp.float32), jax.ShapeDtypeStruct(shape, jnp.bfloat16))
        out_specs = (VMEM, VMEM); out_shape = tuple(pltpu.VMEM(o.shape, o.dtype) for o in out_shape)
    else:
        out_shape = jax.ShapeDtypeStruct((ROWS, tokens, width), jnp.float32)
        out_specs = VMEM; out_shape = pltpu.VMEM(out_shape.shape, out_shape.dtype)
    operands = list(rows) + [weight] + ([start] if has_start else [])
    return pl.pallas_call(
        kernel,
        in_specs=[SMEM] + [VMEM] * len(operands),
        out_specs=out_specs,
        out_shape=out_shape,
        scratch_shapes=[pltpu.VMEM((count, width), jnp.bfloat16)],
        compiler_params=pltpu.CompilerParams(vmem_limit_bytes=12 << 20),
    )(where, *[pltpu.with_memory_space_constraint(o, pltpu.VMEM) for o in operands])


def per_device(inputs, enc_weight, enc_bias, dec_weight, dec_bias):
    decoders = jnp.swapaxes(dec_weight[0], 1, 2)
    sec = lax.axis_index("sec")
    feat = lax.axis_index("feat")
    row = lax.axis_index("row")
    core, chip = feat & 1, feat >> 1

    where = jnp.stack([core, chip, row]).astype(jnp.int32)

    lent = jnp.where(sec == 3, 1, 0)
    lent_a = lax.ppermute(lax.dynamic_index_in_dim(decoders, lent, 0, keepdims=False), "sec", [(2, 0), (3, 1)])
    lent_b = lax.ppermute(decoders[2], "sec", [(3, 2)])

    whole = gather_inputs(inputs[0].T, core, chip)
    features = encode(whole, enc_weight[0], enc_bias)

    every_own = gather_rows(features)
    brought_a = lax.ppermute(features, "sec", [(0, 1), (1, 2)])
    brought_b = lax.ppermute(features, "sec", [(0, 3)])
    every_brought = gather_rows(brought_a + brought_b)

    mine, theirs = decode(where, every_own, lent_a + lent_b, None, "absolute")
    pair = mine + lax.ppermute(theirs, "feat", SWAP).astype(jnp.float32)
    same_core = [[2 * i + c for i in range(CHIPS)] for c in range(2)]
    spread = lax.all_to_all(pair.astype(jnp.bfloat16), "feat", 0, 0, tiled=True, axis_index_groups=same_core)
    lent_sum = jnp.sum(spread.astype(jnp.float32), axis=0)
    back_a = lax.ppermute(lent_sum, "sec", [(0, 2), (1, 3)])
    back_b = lax.ppermute(lent_sum, "sec", [(2, 3)])

    own_weight = lax.dynamic_index_in_dim(decoders, sec, 0, keepdims=False)
    brought_weight = lax.dynamic_index_in_dim(decoders, jnp.where(sec == 2, 1, 0), 0, keepdims=False)
    start = decode(where, every_own, own_weight, None, "")
    mine, theirs = decode(where, every_brought, brought_weight, start, "relative")
    pair = mine + lax.ppermute(theirs, "feat", SWAP).astype(jnp.float32)
    send = pair.astype(jnp.bfloat16)
    got = [lax.ppermute(send[d], "feat", hop(d)) for d in (4, 3, 5, 2, 6, 1, 7)]
    total = pair[0]
    for g in got:
        total = total + g.astype(jnp.float32)
    return (total + back_a + back_b + dec_bias[0]).astype(jnp.bfloat16)[None]


def solution(mesh):
    in_specs = (
        P("sec", "row", "feat"),
        P("sec", None, "feat"),
        P("sec", "feat"),
        P("sec", None, "feat", "row"),
        P("sec", "row"),
    )
    out_specs = P("sec", "feat", "row")

    return jax.shard_map(per_device, mesh=mesh, in_specs=in_specs, out_specs=out_specs, check_vma=False)
```

```python
import jax
import jax.numpy as jnp
from jax import lax
from jax.experimental import pallas as pl
from jax.experimental.pallas import tpu as pltpu
from jax.sharding import PartitionSpec as P


CHIPS = 8
ROWS = 4
PIECE = 64
ANY = pl.BlockSpec(memory_space=pl.ANY)
VMEM = pl.BlockSpec(memory_space=pltpu.VMEM)
SMEM = pl.BlockSpec(memory_space=pltpu.SMEM)
PARAMS = pltpu.CompilerParams(vmem_limit_bytes=12 << 20)


def ring(shift):
    return [(i, (i + shift) % ROWS) for i in range(ROWS)]


def hop(shift):
    return [(i, ((i // 2 + shift) % CHIPS) * 2 + i % 2) for i in range(2 * CHIPS)]


SWAP = [(i, i ^ 1) for i in range(2 * CHIPS)]
BOTH = [(i, ((i // 2 + (1 if i % 2 == 0 else -1)) % CHIPS) * 2 + i % 2) for i in range(2 * CHIPS)]


def in_vmem(values):
    return [pltpu.with_memory_space_constraint(v, pltpu.VMEM) for v in values]


def call(kernel, where, vmem, rest, out, scratch):
    return pl.pallas_call(
        kernel,
        in_specs=[SMEM] + [VMEM] * len(vmem) + [ANY] * len(rest),
        out_specs=tuple(VMEM for _ in out),
        out_shape=tuple(pltpu.VMEM(shape, dtype) for shape, dtype in out),
        scratch_shapes=scratch,
        compiler_params=PARAMS,
    )(where, *in_vmem(vmem), *rest)


def copy_lent(where, decoders):
    _, width, count = decoders.shape

    def kernel(where_ref, source, a_ref, b_ref, sems):
        first = pltpu.make_async_copy(source.at[where_ref[3]], a_ref, sems.at[0])
        second = pltpu.make_async_copy(source.at[2], b_ref, sems.at[1])
        first.start()
        second.start()
        first.wait()
        second.wait()

    out = [((width, count), decoders.dtype)] * 2
    return call(kernel, where, [], [decoders], out, [pltpu.SemaphoreType.DMA((2,))])


def encode(where, pieces, shifts, weight, start, bias):
    size = 2 * weight.shape[0] // (2 * CHIPS)
    tokens = pieces[0].shape[1]
    width = weight.shape[1]
    count = len(shifts)
    vmem = list(pieces) + ([start] if start is not None else []) + ([bias] if bias is not None else [])

    def kernel(where_ref, *refs):
        pieces_refs, refs = refs[: len(pieces)], refs[len(pieces) :]
        if start is not None:
            start_ref, *refs = refs
        if bias is not None:
            bias_ref, *refs = refs
        weight_ref, out_ref, rows, sems = refs
        sign = 1 - 2 * where_ref[0]
        copies = []
        for i, shift in enumerate(shifts):
            at = (where_ref[1] + sign * shift) & (CHIPS - 1)
            copies.append(
                pltpu.make_async_copy(
                    weight_ref.at[pl.ds(pl.multiple_of(at * size, 16), size)],
                    rows.at[pl.ds(i * size, size)],
                    sems.at[i],
                )
            )
        for copy in copies:
            copy.start()
        block = jnp.concatenate([p[...] for p in pieces_refs]).T
        for copy in copies:
            copy.wait()
        hidden = jnp.dot(block, rows[...], preferred_element_type=jnp.float32)
        if start is not None:
            hidden = hidden + start_ref[...]
        if bias is not None:
            hidden = jnp.maximum(hidden + bias_ref[...], 0.0)
        out_ref[...] = hidden.astype(out_ref.dtype)

    out = [((tokens, width), jnp.float32 if bias is None else jnp.bfloat16)]
    scratch = [pltpu.VMEM((count * size, width), weight.dtype), pltpu.SemaphoreType.DMA((count,))]
    return call(kernel, where, vmem, [weight], out, scratch)[0]


def gather_and_encode(where, core, own, weight, bias):
    other = lax.ppermute(own, "feat", SWAP)
    block = jnp.where(core == 0, jnp.concatenate([own, other]), jnp.concatenate([other, own]))
    b1 = lax.ppermute(block, "feat", BOTH)
    b2 = lax.ppermute(b1, "feat", BOTH)
    s1 = lax.ppermute(b1, "feat", SWAP)
    b3 = lax.ppermute(b2, "feat", BOTH)
    s2 = lax.ppermute(b2, "feat", SWAP)
    sums = encode(where, [block, b1, s1], (0, -1, 1), weight, None, None)
    b4 = lax.ppermute(b3, "feat", BOTH)
    s3 = lax.ppermute(b3, "feat", SWAP)
    sums = encode(where, [b2, s2, b3], (-2, 2, -3), weight, sums, None)
    return encode(where, [s3, b4], (3, -4), weight, sums, bias)


def gather_rows(own):
    half = own.shape[0] // 2
    before = lax.ppermute(own, "row", ring(1))
    after = lax.ppermute(own, "row", ring(-1))
    first = lax.ppermute(before[:half], "row", ring(1))
    second = lax.ppermute(after[half:], "row", ring(-1))
    return own, before, after, first, second


def decode(where, rows, weights, start, split):
    tokens, count = rows[0].shape
    width = weights[0].shape[0]
    n = len(weights)
    has_start = start is not None

    def kernel(where_ref, own, before, after, first, second, *rest):
        core, chip, row = where_ref[0], where_ref[1], where_ref[2]
        weight = rest[0][...]
        for other in rest[1:n]:
            weight = weight + other[...]
        rest = rest[n:]
        if has_start:
            start_ref, *rest = rest
        if split:
            mine_ref, theirs_ref, turned = rest
        else:
            out_ref, turned = rest
        turned[...] = weight.T
        for j, parts in enumerate(((own,), (after,), (first, second), (before,))):
            block = parts[0][...] if len(parts) == 1 else jnp.concatenate([p[...] for p in parts])
            value = jnp.dot(block, turned[...], preferred_element_type=jnp.float32)
            if has_start:
                value = value + start_ref[j]
            if not split:
                out_ref[j] = value
                continue
            for h in range(2):
                at = (2 * ((row + j) & (ROWS - 1)) + h - chip) & (CHIPS - 1)
                low = value[2 * h * PIECE : (2 * h + 1) * PIECE]
                high = value[(2 * h + 1) * PIECE : (2 * h + 2) * PIECE]
                mine_ref[at] = jnp.where(core == 0, low, high)
                theirs_ref[at] = jnp.where(core == 0, high, low).astype(jnp.bfloat16)

    if split:
        shape = (CHIPS, PIECE, width)
        out = [(shape, jnp.float32), (shape, jnp.bfloat16)]
    else:
        out = [((ROWS, tokens, width), jnp.float32)]
    vmem = list(rows) + list(weights) + ([start] if has_start else [])
    return call(kernel, where, vmem, [], out, [pltpu.VMEM((count, width), jnp.bfloat16)])


def per_device(inputs, enc_weight, enc_bias, dec_weight, dec_bias):
    decoders = jnp.swapaxes(dec_weight[0], 1, 2)
    sec = lax.axis_index("sec")
    feat = lax.axis_index("feat")
    row = lax.axis_index("row")
    core, chip = feat & 1, feat >> 1
    where = jnp.stack([core, chip, row, jnp.where(sec == 3, 1, 0)]).astype(jnp.int32)

    lent_a, lent_b = copy_lent(where, decoders)
    lent_a = lax.ppermute(lent_a, "sec", [(2, 0), (3, 1)])
    lent_b = lax.ppermute(lent_b, "sec", [(3, 2)])

    features = gather_and_encode(where, core, inputs[0].T, enc_weight[0], enc_bias)

    every_own = gather_rows(features)
    brought_a = lax.ppermute(features, "sec", [(0, 1), (1, 2)])
    brought_b = lax.ppermute(features, "sec", [(0, 3)])
    every_brought = gather_rows(brought_a + brought_b)

    mine, theirs = decode(where, every_own, (lent_a, lent_b), None, True)
    pair = mine + lax.ppermute(theirs, "feat", SWAP).astype(jnp.float32)
    pair = pair.astype(jnp.bfloat16)
    back_a = lax.ppermute(pair, "sec", [(0, 2), (1, 3)])
    back_b = lax.ppermute(pair, "sec", [(2, 3)])

    late, _ = lax.optimization_barrier((decoders, features))
    own_weight = lax.dynamic_index_in_dim(late, sec, 0, keepdims=False)
    brought_weight = lax.dynamic_index_in_dim(late, jnp.where(sec == 2, 1, 0), 0, keepdims=False)
    (start,) = decode(where, every_own, (own_weight,), None, False)
    mine, theirs = decode(where, every_brought, (brought_weight,), start, True)
    pair = mine + lax.ppermute(theirs, "feat", SWAP).astype(jnp.float32)
    pair = pair + back_a.astype(jnp.float32) + back_b.astype(jnp.float32)
    send = pair.astype(jnp.bfloat16)
    got = [lax.ppermute(send[d], "feat", hop(d)) for d in (4, 3, 5, 2, 6, 1, 7)]
    total = pair[0]
    for g in got:
        total = total + g.astype(jnp.float32)
    return (total + dec_bias[0]).astype(jnp.bfloat16)[None]


def solution(mesh):
    in_specs = (
        P("sec", "row", "feat"),
        P("sec", None, "feat"),
        P("sec", "feat"),
        P("sec", None, "feat", "row"),
        P("sec", "row"),
    )
    out_specs = P("sec", "feat", "row")

    return jax.shard_map(per_device, mesh=mesh, in_specs=in_specs, out_specs=out_specs, check_vma=False)
```

```python
import jax
import jax.numpy as jnp
from jax import lax
from jax.experimental import pallas as pl
from jax.experimental.pallas import tpu as pltpu
from jax.sharding import PartitionSpec as P


CHIPS = 8
ROWS = 4
PIECE = 64
ANY = pl.BlockSpec(memory_space=pl.ANY)
VMEM = pl.BlockSpec(memory_space=pltpu.VMEM)
SMEM = pl.BlockSpec(memory_space=pltpu.SMEM)
PARAMS = pltpu.CompilerParams(vmem_limit_bytes=12 << 20)


def ring(shift, sections=(0, 1, 2, 3)):
    return [(s * ROWS + i, s * ROWS + (i + shift) % ROWS) for s in sections for i in range(ROWS)]


def hop(shift):
    return [(i, ((i // 2 + shift) % CHIPS) * 2 + i % 2) for i in range(2 * CHIPS)]


SWAP = [(i, i ^ 1) for i in range(2 * CHIPS)]
BOTH = [(i, ((i // 2 + (1 if i % 2 == 0 else -1)) % CHIPS) * 2 + i % 2) for i in range(2 * CHIPS)]


def in_vmem(values):
    return [pltpu.with_memory_space_constraint(v, pltpu.VMEM) for v in values]


def call(kernel, where, vmem, rest, out, scratch):
    return pl.pallas_call(
        kernel,
        in_specs=[SMEM] + [VMEM] * len(vmem) + [ANY] * len(rest),
        out_specs=tuple(VMEM for _ in out),
        out_shape=tuple(pltpu.VMEM(shape, dtype) for shape, dtype in out),
        scratch_shapes=scratch,
        compiler_params=PARAMS,
    )(where, *in_vmem(vmem), *rest)


def copy_lent(where, decoders):
    _, width, count = decoders.shape

    def kernel(where_ref, source, a_ref, b_ref, sems):
        first = pltpu.make_async_copy(source.at[where_ref[3]], a_ref, sems.at[0])
        second = pltpu.make_async_copy(source.at[2], b_ref, sems.at[1])
        first.start()
        second.start()
        first.wait()
        second.wait()

    out = [((width, count), decoders.dtype)] * 2
    decoders = pltpu.with_memory_space_constraint(decoders, pltpu.HBM)
    return call(kernel, where, [], [decoders], out, [pltpu.SemaphoreType.DMA((2,))])


def encode(where, pieces, shifts, weight, start, bias):
    size = 2 * weight.shape[0] // (2 * CHIPS)
    tokens = pieces[0].shape[1]
    width = weight.shape[1]
    count = len(shifts)
    vmem = list(pieces) + ([start] if start is not None else []) + ([bias] if bias is not None else [])

    def kernel(where_ref, *refs):
        pieces_refs, refs = refs[: len(pieces)], refs[len(pieces) :]
        if start is not None:
            start_ref, *refs = refs
        if bias is not None:
            bias_ref, *refs = refs
        weight_ref, out_ref, rows, sems = refs
        sign = 1 - 2 * where_ref[0]
        copies = []
        for i, shift in enumerate(shifts):
            at = (where_ref[1] + sign * shift) & (CHIPS - 1)
            copies.append(
                pltpu.make_async_copy(
                    weight_ref.at[pl.ds(pl.multiple_of(at * size, 16), size)],
                    rows.at[pl.ds(i * size, size)],
                    sems.at[i],
                )
            )
        for copy in copies:
            copy.start()
        block = jnp.concatenate([p[...] for p in pieces_refs]).T
        for copy in copies:
            copy.wait()
        hidden = jnp.dot(block, rows[...], preferred_element_type=jnp.float32)
        if start is not None:
            hidden = hidden + start_ref[...]
        if bias is not None:
            hidden = jnp.maximum(hidden + bias_ref[...], 0.0)
        out_ref[...] = hidden.astype(out_ref.dtype)

    out = [((tokens, width), jnp.float32 if bias is None else jnp.bfloat16)]
    scratch = [pltpu.VMEM((count * size, width), weight.dtype), pltpu.SemaphoreType.DMA((count,))]
    return call(kernel, where, vmem, [weight], out, scratch)[0]


def gather_and_encode(where, core, own, weight, bias):
    other = lax.ppermute(own, "feat", SWAP)
    block = jnp.where(core == 0, jnp.concatenate([own, other]), jnp.concatenate([other, own]))
    b1 = lax.ppermute(block, "feat", BOTH)
    b2 = lax.ppermute(b1, "feat", BOTH)
    s1 = lax.ppermute(b1, "feat", SWAP)
    b3 = lax.ppermute(b2, "feat", BOTH)
    s2 = lax.ppermute(b2, "feat", SWAP)
    sums = encode(where, [block, b1, s1], (0, -1, 1), weight, None, None)
    b4 = lax.ppermute(b3, "feat", BOTH)
    s3 = lax.ppermute(b3, "feat", SWAP)
    sums = encode(where, [b2, s2, b3], (-2, 2, -3), weight, sums, None)
    return encode(where, [s3, b4], (3, -4), weight, sums, bias)


def gather_rows(own, sections):
    half = own.shape[0] // 2
    axes = ("sec", "row")
    before = lax.ppermute(own, axes, ring(1, sections))
    after = lax.ppermute(own, axes, ring(-1, sections))
    first = lax.ppermute(before[:half], axes, ring(1, sections))
    second = lax.ppermute(after[half:], axes, ring(-1, sections))
    return own, before, after, first, second


def decode(where, rows, weights, start, split, only=None):
    tokens, count = rows[0].shape
    width = weights[0].shape[0]
    n = len(weights)
    has_start = start is not None

    def kernel(where_ref, own, before, after, first, second, *rest):
        if only is None:
            work(where_ref, own, before, after, first, second, *rest)
        else:

            @pl.when(where_ref[4] == only)
            def _():
                work(where_ref, own, before, after, first, second, *rest)

    def work(where_ref, own, before, after, first, second, *rest):
        core, chip, row = where_ref[0], where_ref[1], where_ref[2]
        weight = rest[0][...]
        for other in rest[1:n]:
            weight = weight + other[...]
        rest = rest[n:]
        if has_start:
            start_ref, *rest = rest
        if split:
            mine_ref, theirs_ref, turned = rest
        else:
            out_ref, turned = rest
        turned[...] = weight.T
        for j, parts in enumerate(((own,), (after,), (first, second), (before,))):
            block = parts[0][...] if len(parts) == 1 else jnp.concatenate([p[...] for p in parts])
            value = jnp.dot(block, turned[...], preferred_element_type=jnp.float32)
            if has_start:
                value = value + start_ref[j]
            if not split:
                out_ref[j] = value
                continue
            for h in range(2):
                at = (2 * ((row + j) & (ROWS - 1)) + h - chip) & (CHIPS - 1)
                low = value[2 * h * PIECE : (2 * h + 1) * PIECE]
                high = value[(2 * h + 1) * PIECE : (2 * h + 2) * PIECE]
                mine_ref[at] = jnp.where(core == 0, low, high)
                theirs_ref[at] = jnp.where(core == 0, high, low).astype(jnp.bfloat16)

    if split:
        shape = (CHIPS, PIECE, width)
        out = [(shape, jnp.float32), (shape, jnp.bfloat16)]
    else:
        out = [((ROWS, tokens, width), jnp.float32)]
    vmem = list(rows) + list(weights) + ([start] if has_start else [])
    return call(kernel, where, vmem, [], out, [pltpu.VMEM((count, width), jnp.bfloat16)])


def per_device(inputs, enc_weight, enc_bias, dec_weight, dec_bias):
    decoders = jnp.swapaxes(dec_weight[0], 1, 2)
    sec = lax.axis_index("sec")
    feat = lax.axis_index("feat")
    row = lax.axis_index("row")
    core, chip = feat & 1, feat >> 1
    where = jnp.stack([core, chip, row, jnp.where(sec == 2, 1, 0), sec]).astype(jnp.int32)

    lent_a, lent_b = copy_lent(where, decoders)
    lent_c = lax.ppermute(lent_a, "sec", [(1, 0)])
    lent_a = lax.ppermute(lent_a, "sec", [(2, 1), (3, 0)])
    lent_b = lax.ppermute(lent_b, "sec", [(3, 2)])

    features = gather_and_encode(where, core, inputs[0].T, enc_weight[0], enc_bias)

    every_own = gather_rows(features, (0, 1, 2, 3))
    brought = lax.ppermute(features, "sec", [(0, 2), (1, 3)])
    every_brought = gather_rows(brought, (2, 3))

    mine, theirs = decode(where, every_own, (lent_a, lent_b), None, True)
    pair = mine + lax.ppermute(theirs, "feat", SWAP).astype(jnp.float32)
    pair = pair.astype(jnp.bfloat16)
    back_a = lax.ppermute(pair, "sec", [(0, 3), (1, 2)])
    back_b = lax.ppermute(pair, "sec", [(2, 3)])
    mine, theirs = decode(where, every_own, (lent_c,), None, True, only=0)
    pair = mine + lax.ppermute(theirs, ("sec", "feat"), SWAP).astype(jnp.float32)
    back_c = lax.ppermute(pair.astype(jnp.bfloat16), "sec", [(0, 1)])

    late, _ = lax.optimization_barrier((decoders, features))
    own_weight = lax.dynamic_index_in_dim(late, sec, 0, keepdims=False)
    brought_weight = lax.dynamic_index_in_dim(late, jnp.where(sec == 3, 1, 0), 0, keepdims=False)
    (start,) = decode(where, every_own, (own_weight,), None, False)
    mine, theirs = decode(where, every_brought, (brought_weight,), start, True)
    pair = mine + lax.ppermute(theirs, "feat", SWAP).astype(jnp.float32)
    for back in (back_a, back_b, back_c):
        pair = pair + back.astype(jnp.float32)
    send = pair.astype(jnp.bfloat16)
    got = [lax.ppermute(send[d], "feat", hop(d)) for d in (4, 3, 5, 2, 6, 1, 7)]
    total = pair[0]
    for g in got:
        total = total + g.astype(jnp.float32)
    return (total + dec_bias[0]).astype(jnp.bfloat16)[None]


def solution(mesh):
    in_specs = (
        P("sec", "row", "feat"),
        P("sec", None, "feat"),
        P("sec", "feat"),
        P("sec", None, "feat", "row"),
        P("sec", "row"),
    )
    out_specs = P("sec", "feat", "row")

    return jax.shard_map(per_device, mesh=mesh, in_specs=in_specs, out_specs=out_specs, check_vma=False)
```

```python
import jax
import jax.numpy as jnp
from jax import lax
from jax.experimental import pallas as pl
from jax.experimental.pallas import tpu as pltpu
from jax.sharding import PartitionSpec as P


CHIPS = 8
ROWS = 4
PIECE = 64
ANY = pl.BlockSpec(memory_space=pl.ANY)
VMEM = pl.BlockSpec(memory_space=pltpu.VMEM)
SMEM = pl.BlockSpec(memory_space=pltpu.SMEM)
PARAMS = pltpu.CompilerParams(vmem_limit_bytes=12 << 20)


def ring(shift):
    return [(i, (i + shift) % ROWS) for i in range(ROWS)]


def hop(shift):
    return [(i, ((i // 2 + shift) % CHIPS) * 2 + i % 2) for i in range(2 * CHIPS)]


SWAP = [(i, i ^ 1) for i in range(2 * CHIPS)]


def both(shift):
    return [(i, ((i // 2 + (shift if i % 2 == 0 else -shift)) % CHIPS) * 2 + i % 2) for i in range(2 * CHIPS)]


def in_vmem(values):
    return [pltpu.with_memory_space_constraint(v, pltpu.VMEM) for v in values]


def call(kernel, where, vmem, rest, out, scratch):
    return pl.pallas_call(
        kernel,
        in_specs=[SMEM] + [VMEM] * len(vmem) + [ANY] * len(rest),
        out_specs=tuple(VMEM for _ in out),
        out_shape=tuple(pltpu.VMEM(shape, dtype) for shape, dtype in out),
        scratch_shapes=scratch,
        compiler_params=PARAMS,
    )(where, *in_vmem(vmem), *rest)


def copy_weights(where, decoders, picks):
    _, width, count = decoders.shape
    n = len(picks)

    def kernel(where_ref, source, *refs):
        third = width // 3
        copies = [
            pltpu.make_async_copy(
                source.at[where_ref[pick], pl.ds(part * third, third)],
                refs[i].at[pl.ds(part * third, third)],
                refs[n].at[3 * i + part],
            )
            for i, pick in enumerate(picks)
            for part in range(3)
        ]
        for copy in copies:
            copy.start()
        for copy in copies:
            copy.wait()

    out = [((width, count), decoders.dtype)] * n
    decoders = pltpu.with_memory_space_constraint(decoders, pltpu.HBM)
    return call(kernel, where, [], [decoders], out, [pltpu.SemaphoreType.DMA((3 * n,))])


def encode(where, pieces, shifts, weight, start, bias):
    size = 2 * weight.shape[0] // (2 * CHIPS)
    tokens = pieces[0].shape[1]
    width = weight.shape[1]
    count = len(shifts)
    vmem = list(pieces) + ([start] if start is not None else []) + ([bias] if bias is not None else [])

    def kernel(where_ref, *refs):
        pieces_refs, refs = refs[: len(pieces)], refs[len(pieces) :]
        if start is not None:
            start_ref, *refs = refs
        if bias is not None:
            bias_ref, *refs = refs
        weight_ref, out_ref, rows, sems = refs
        sign = 1 - 2 * where_ref[0]
        copies = []
        for i, shift in enumerate(shifts):
            at = (where_ref[1] + sign * shift) & (CHIPS - 1)
            copies.append(
                pltpu.make_async_copy(
                    weight_ref.at[pl.ds(pl.multiple_of(at * size, 16), size)],
                    rows.at[pl.ds(i * size, size)],
                    sems.at[i],
                )
            )
        for copy in copies:
            copy.start()
        block = jnp.concatenate([p[...] for p in pieces_refs]).T
        for copy in copies:
            copy.wait()
        hidden = jnp.dot(block, rows[...], preferred_element_type=jnp.float32)
        if start is not None:
            hidden = hidden + start_ref[...]
        if bias is not None:
            hidden = jnp.maximum(hidden + bias_ref[...], 0.0)
        out_ref[...] = hidden.astype(out_ref.dtype)

    out = [((tokens, width), jnp.float32 if bias is None else jnp.bfloat16)]
    scratch = [pltpu.VMEM((count * size, width), weight.dtype), pltpu.SemaphoreType.DMA((count,))]
    return call(kernel, where, vmem, [weight], out, scratch)[0]


def gather_and_encode(where, core, own, weight, bias):
    other = lax.ppermute(own, "feat", SWAP)
    block = jnp.where(core == 0, jnp.concatenate([own, other]), jnp.concatenate([other, own]))
    b1 = lax.ppermute(block, "feat", both(1))
    b2 = lax.ppermute(block, "feat", both(2))
    b3 = lax.ppermute(b1, "feat", both(2))
    b4 = lax.ppermute(b2, "feat", both(2))
    s1 = lax.ppermute(b1, "feat", SWAP)
    s2 = lax.ppermute(b2, "feat", SWAP)
    s3 = lax.ppermute(b3, "feat", SWAP)
    sums = encode(where, [block, b1, s1], (0, -1, 1), weight, None, None)
    sums = encode(where, [b2, s2, b3], (-2, 2, -3), weight, sums, None)
    return encode(where, [s3, b4], (3, -4), weight, sums, bias)


def gather_rows(own):
    half = own.shape[0] // 2
    before = lax.ppermute(own, "row", ring(1))
    after = lax.ppermute(own, "row", ring(-1))
    before_half, after_half = before[:half], after[half:]
    first = lax.ppermute(before_half, "row", ring(1))
    second = lax.ppermute(after_half, "row", ring(-1))
    return own, before, after, first, second


def decode(where, rows, weights, start, split, only=None):
    tokens, count = rows[0].shape
    width = weights[0].shape[0]
    n = len(weights)
    has_start = start is not None

    def kernel(where_ref, own, before, after, first, second, *rest):
        if only is None:
            work(where_ref, own, before, after, first, second, *rest)
        else:

            @pl.when(where_ref[4] == only)
            def _():
                work(where_ref, own, before, after, first, second, *rest)

    def work(where_ref, own, before, after, first, second, *rest):
        core, chip, row = where_ref[0], where_ref[1], where_ref[2]
        weight = rest[0][...]
        for other in rest[1:n]:
            weight = weight + other[...]
        rest = rest[n:]
        if has_start:
            start_ref, *rest = rest
        if split:
            mine_ref, theirs_ref, turned = rest
        else:
            out_ref, turned = rest
        turned[...] = weight.T
        for j, parts in enumerate(((own,), (after,), (first, second), (before,))):
            block = parts[0][...] if len(parts) == 1 else jnp.concatenate([p[...] for p in parts])
            value = jnp.dot(block, turned[...], preferred_element_type=jnp.float32)
            if has_start:
                value = value + start_ref[j]
            if not split:
                out_ref[j] = value
                continue
            for h in range(2):
                at = (2 * ((row + j) & (ROWS - 1)) + h - chip) & (CHIPS - 1)
                low = value[2 * h * PIECE : (2 * h + 1) * PIECE]
                high = value[(2 * h + 1) * PIECE : (2 * h + 2) * PIECE]
                mine_ref[at] = jnp.where(core == 0, low, high)
                theirs_ref[at] = jnp.where(core == 0, high, low).astype(jnp.bfloat16)

    if split:
        shape = (CHIPS, PIECE, width)
        out = [(shape, jnp.float32), (shape, jnp.bfloat16)]
    else:
        out = [((ROWS, tokens, width), jnp.float32)]
    vmem = list(rows) + list(weights) + ([start] if has_start else [])
    return call(kernel, where, vmem, [], out, [pltpu.VMEM((count, width), jnp.bfloat16)])


def per_device(inputs, enc_weight, enc_bias, dec_weight, dec_bias):
    decoders = jnp.swapaxes(dec_weight[0], 1, 2)
    sec = lax.axis_index("sec")
    feat = lax.axis_index("feat")
    row = lax.axis_index("row")
    core, chip = feat & 1, feat >> 1
    where = jnp.stack([core, chip, row, jnp.where(sec == 2, 1, 0), sec, jnp.where(sec == 3, 1, 0), 2])
    where = where.astype(jnp.int32)

    lent_a, lent_b = copy_weights(where, decoders, (3, 6))
    lent_c = lax.ppermute(lent_a, "sec", [(1, 0)])
    lent_a = lax.ppermute(lent_a, "sec", [(2, 1), (3, 0)])
    lent_b = lax.ppermute(lent_b, "sec", [(3, 2)])

    features = gather_and_encode(where, core, inputs[0].T, enc_weight[0], enc_bias)

    every_own = gather_rows(features)
    brought = lax.ppermute(features, "sec", [(0, 2), (1, 3)])
    every_brought = gather_rows(brought)

    mine, theirs = decode(where, every_own, (lent_a, lent_b), None, True)
    pair = mine + lax.ppermute(theirs, "feat", SWAP).astype(jnp.float32)
    pair = pair.astype(jnp.bfloat16)
    back_a = lax.ppermute(pair, "sec", [(0, 3), (1, 2)])
    back_b = lax.ppermute(pair, "sec", [(2, 3)])
    mine, theirs = decode(where, every_own, (lent_c,), None, True, only=0)
    pair = mine + lax.ppermute(theirs, ("sec", "feat"), SWAP).astype(jnp.float32)
    back_c = lax.ppermute(pair.astype(jnp.bfloat16), "sec", [(0, 1)])

    own_weight, brought_weight = copy_weights(where, decoders, (4, 5))
    (start,) = decode(where, every_own, (own_weight,), None, False)
    mine, theirs = decode(where, every_brought, (brought_weight,), start, True)
    pair = mine + lax.ppermute(theirs, "feat", SWAP).astype(jnp.float32)
    for back in (back_a, back_b, back_c):
        pair = pair + back.astype(jnp.float32)
    send = pair.astype(jnp.bfloat16)
    up = lax.ppermute(jnp.stack([send[4], send[2]]), "feat", hop(1))
    down = lax.ppermute(send[6], "feat", hop(-1))
    got = [lax.ppermute(send[5], "feat", hop(-3))]
    for piece, extra, shift in ((3, up[0], 3), (1, up[1], 1), (7, down, -1)):
        merged = (pair[piece] + extra.astype(jnp.float32)).astype(jnp.bfloat16)
        got.append(lax.ppermute(merged, "feat", hop(shift)))
    total = pair[0]
    for g in got:
        total = total + g.astype(jnp.float32)
    return (total + dec_bias[0]).astype(jnp.bfloat16)[None]


def solution(mesh):
    in_specs = (
        P("sec", "row", "feat"),
        P("sec", None, "feat"),
        P("sec", "feat"),
        P("sec", None, "feat", "row"),
        P("sec", "row"),
    )
    out_specs = P("sec", "feat", "row")

    return jax.shard_map(per_device, mesh=mesh, in_specs=in_specs, out_specs=out_specs, check_vma=False)
```

```python
import jax
import jax.numpy as jnp
from jax import lax
from jax.experimental import pallas as pl
from jax.experimental.pallas import tpu as pltpu
from jax.sharding import PartitionSpec as P


CHIPS = 8
ROWS = 4
PIECE = 64
ANY = pl.BlockSpec(memory_space=pl.ANY)
VMEM = pl.BlockSpec(memory_space=pltpu.VMEM)
SMEM = pl.BlockSpec(memory_space=pltpu.SMEM)
PARAMS = pltpu.CompilerParams(vmem_limit_bytes=12 << 20)


def ring(shift):
    return [(i, (i + shift) % ROWS) for i in range(ROWS)]


def hop(shift):
    return [(i, ((i // 2 + shift) % CHIPS) * 2 + i % 2) for i in range(2 * CHIPS)]


SWAP = [(i, i ^ 1) for i in range(2 * CHIPS)]


def both(shift):
    return [(i, ((i // 2 + (shift if i % 2 == 0 else -shift)) % CHIPS) * 2 + i % 2) for i in range(2 * CHIPS)]


def in_vmem(values):
    return [pltpu.with_memory_space_constraint(v, pltpu.VMEM) for v in values]


def call(kernel, where, vmem, rest, out, scratch, aliases=None):
    return pl.pallas_call(
        kernel,
        in_specs=[SMEM] + [VMEM] * len(vmem) + [ANY] * len(rest),
        out_specs=tuple(VMEM for _ in out),
        out_shape=tuple(pltpu.VMEM(shape, dtype) for shape, dtype in out),
        scratch_shapes=scratch,
        compiler_params=PARAMS,
        input_output_aliases={1 + i: o for i, o in (aliases or {}).items()},
    )(where, *in_vmem(vmem), *rest)


def copy_weights(where, decoders, picks):
    _, width, count = decoders.shape
    n = len(picks)

    def kernel(where_ref, source, *refs):
        third = width // 3
        copies = [
            pltpu.make_async_copy(
                source.at[where_ref[pick], pl.ds(part * third, third)],
                refs[i].at[pl.ds(part * third, third)],
                refs[n].at[3 * i + part],
            )
            for i, pick in enumerate(picks)
            for part in range(3)
        ]
        for copy in copies:
            copy.start()
        for copy in copies:
            copy.wait()

    out = [((width, count), decoders.dtype)] * n
    decoders = pltpu.with_memory_space_constraint(decoders, pltpu.HBM)
    return call(kernel, where, [], [decoders], out, [pltpu.SemaphoreType.DMA((3 * n,))])


def encode(where, pieces, weight, start, bias):
    half = weight.shape[0] // (2 * CHIPS)
    tokens = pieces[0][0].shape[1]
    width = weight.shape[1]
    arrays = [array for array, _ in pieces]
    halves = [place for _, places in pieces for place in places]
    vmem = [weight] + arrays + ([start] if start is not None else []) + ([bias] if bias is not None else [])

    def kernel(where_ref, weight_ref, *refs):
        pieces_refs, refs = refs[: len(arrays)], refs[len(arrays) :]
        if start is not None:
            start_ref, *refs = refs
        if bias is not None:
            bias_ref, *refs = refs
        (out_ref,) = refs
        core = where_ref[0]
        sign = 1 - 2 * core
        rows = []
        for shift, other in halves:
            at = 2 * ((where_ref[1] + sign * shift) & (CHIPS - 1)) + (1 - core if other else core)
            rows.append(weight_ref[pl.ds(pl.multiple_of(at * half, 16), half), :])
        block = jnp.concatenate([p[...] for p in pieces_refs]).T
        hidden = jnp.dot(block, jnp.concatenate(rows), preferred_element_type=jnp.float32)
        if start is not None:
            hidden = hidden + start_ref[...]
        if bias is not None:
            hidden = jnp.maximum(hidden + bias_ref[...], 0.0)
        out_ref[...] = hidden.astype(out_ref.dtype)

    out = [((tokens, width), jnp.float32 if bias is None else jnp.bfloat16)]
    return call(kernel, where, vmem, [], out, [])[0]


def gather_and_encode(where, own, weight, bias):
    other = lax.ppermute(own, "feat", SWAP)
    block = jnp.concatenate([own, other])
    b1 = lax.ppermute(block, "feat", both(1))
    b2 = lax.ppermute(block, "feat", both(2))
    b3 = lax.ppermute(b1, "feat", both(2))
    b4 = lax.ppermute(b2, "feat", both(2))
    s1 = lax.ppermute(b1, "feat", SWAP)
    s2 = lax.ppermute(b2, "feat", SWAP)
    s3 = lax.ppermute(b3, "feat", SWAP)

    def direct(piece, shift):
        return piece, [(shift, 0), (shift, 1)]

    def swapped(piece, shift):
        return piece, [(shift, 1), (shift, 0)]

    first = [direct(block, 0), direct(b1, -1), swapped(s1, 1), direct(b2, -2), swapped(s2, 2)]
    sums = encode(where, first, weight, None, None)
    return encode(where, [direct(b3, -3), swapped(s3, 3), direct(b4, -4)], weight, sums, bias)


def gather_rows(own):
    half = own.shape[0] // 2
    before = lax.ppermute(own, "row", ring(1))
    after = lax.ppermute(own, "row", ring(-1))
    before_half, after_half = before[:half], after[half:]
    first = lax.ppermute(before_half, "row", ring(1))
    second = lax.ppermute(after_half, "row", ring(-1))
    return own, before, after, first, second


def spread(where_ref, value, j, mine_ref, theirs_ref):
    core, chip, row = where_ref[0], where_ref[1], where_ref[2]
    for h in range(2):
        at = (2 * ((row + j) & (ROWS - 1)) + h - chip) & (CHIPS - 1)
        low = value[2 * h * PIECE : (2 * h + 1) * PIECE]
        high = value[(2 * h + 1) * PIECE : (2 * h + 2) * PIECE]
        mine_ref[at] = jnp.where(core == 0, low, high)
        theirs_ref[at] = jnp.where(core == 0, high, low).astype(jnp.bfloat16)


def decode_far(where, rows, turned, start, mine, theirs):
    first, second = rows

    def kernel(where_ref, first, second, turned_ref, start_ref, mine_in, theirs_in, mine_ref, theirs_ref):
        block = jnp.concatenate([first[...], second[...]])
        value = jnp.dot(block, turned_ref[...], preferred_element_type=jnp.float32) + start_ref[2]
        spread(where_ref, value, 2, mine_ref, theirs_ref)

    out = [(mine.shape, mine.dtype), (theirs.shape, theirs.dtype)]
    return call(kernel, where, [first, second, turned, start, mine, theirs], [], out, [], {4: 0, 5: 1})


def decode(where, rows, weights, start, split, only=None):
    tokens, count = rows[0].shape
    width = weights[0].shape[0]
    n = len(weights)
    m = len(rows)
    has_start = start is not None

    def kernel(where_ref, *refs):
        if only is None:
            work(where_ref, *refs)
        else:

            @pl.when(where_ref[4] == only)
            def _():
                work(where_ref, *refs)

    def work(where_ref, *refs):
        own, before, after = refs[:3]
        blocks = [(0, (own,)), (1, (after,)), (3, (before,))] + ([(2, refs[3:m])] if m == 5 else [])
        weight = refs[m][...]
        for other in refs[m + 1 : m + n]:
            weight = weight + other[...]
        rest = refs[m + n :]
        if has_start:
            start_ref, *rest = rest
        if split:
            mine_ref, theirs_ref, turned = rest
        else:
            out_ref, turned = rest
        turned[...] = weight.T
        for j, parts in blocks:
            block = parts[0][...] if len(parts) == 1 else jnp.concatenate([p[...] for p in parts])
            value = jnp.dot(block, turned[...], preferred_element_type=jnp.float32)
            if has_start:
                value = value + start_ref[j]
            if split:
                spread(where_ref, value, j, mine_ref, theirs_ref)
            else:
                out_ref[j] = value

    if split:
        shape = (CHIPS, PIECE, width)
        out = [(shape, jnp.float32), (shape, jnp.bfloat16)]
    else:
        out = [((ROWS, tokens, width), jnp.float32)]
    vmem = list(rows) + list(weights) + ([start] if has_start else [])
    turned = ((count, width), jnp.bfloat16)
    if m == 3:
        return call(kernel, where, vmem, [], out + [turned], [])
    return call(kernel, where, vmem, [], out, [pltpu.VMEM(*turned)])


def per_device(inputs, enc_weight, enc_bias, dec_weight, dec_bias):
    decoders = jnp.swapaxes(dec_weight[0], 1, 2)
    sec = lax.axis_index("sec")
    feat = lax.axis_index("feat")
    row = lax.axis_index("row")
    core, chip = feat & 1, feat >> 1
    where = jnp.stack([core, chip, row, jnp.where(sec == 2, 1, 0), sec, jnp.where(sec == 3, 1, 0), 2])
    where = where.astype(jnp.int32)

    lent_a, lent_b = copy_weights(where, decoders, (3, 6))
    lent_c = lax.ppermute(lent_a, "sec", [(1, 0)])
    lent_a = lax.ppermute(lent_a, "sec", [(2, 1), (3, 0)])
    lent_b = lax.ppermute(lent_b, "sec", [(3, 2)])

    features = gather_and_encode(where, inputs[0].T, enc_weight[0], enc_bias)

    every_own = gather_rows(features)
    brought = lax.ppermute(features, "sec", [(0, 2), (1, 3)])
    every_brought = gather_rows(brought)

    mine, theirs = decode(where, every_own, (lent_a, lent_b), None, True)
    pair = mine + lax.ppermute(theirs, "feat", SWAP).astype(jnp.float32)
    pair = pair.astype(jnp.bfloat16)
    back_a = lax.ppermute(pair, "sec", [(0, 3), (1, 2)])
    back_b = lax.ppermute(pair, "sec", [(2, 3)])
    mine, theirs = decode(where, every_own, (lent_c,), None, True, only=0)
    pair = mine + lax.ppermute(theirs, ("sec", "feat"), SWAP).astype(jnp.float32)
    back_c = lax.ppermute(pair.astype(jnp.bfloat16), "sec", [(0, 1)])

    own_weight, brought_weight = copy_weights(where, decoders, (4, 5))
    (start,) = decode(where, every_own, (own_weight,), None, False)
    mine, theirs, turned = decode(where, every_brought[:3], (brought_weight,), start, True)
    mine, theirs = decode_far(where, every_brought[3:], turned, start, mine, theirs)
    pair = mine + lax.ppermute(theirs, "feat", SWAP).astype(jnp.float32)
    for back in (back_a, back_b, back_c):
        pair = pair + back.astype(jnp.float32)
    send = pair.astype(jnp.bfloat16)
    up = lax.ppermute(jnp.stack([send[4], send[2]]), "feat", hop(1))
    down = lax.ppermute(send[6], "feat", hop(-1))
    got = [lax.ppermute(send[5], "feat", hop(-3))]
    for piece, extra, shift in ((3, up[0], 3), (1, up[1], 1), (7, down, -1)):
        merged = (pair[piece] + extra.astype(jnp.float32)).astype(jnp.bfloat16)
        got.append(lax.ppermute(merged, "feat", hop(shift)))
    total = pair[0]
    for g in got:
        total = total + g.astype(jnp.float32)
    return (total + dec_bias[0]).astype(jnp.bfloat16)[None]


def solution(mesh):
    in_specs = (
        P("sec", "row", "feat"),
        P("sec", None, "feat"),
        P("sec", "feat"),
        P("sec", None, "feat", "row"),
        P("sec", "row"),
    )
    out_specs = P("sec", "feat", "row")

    return jax.shard_map(per_device, mesh=mesh, in_specs=in_specs, out_specs=out_specs, check_vma=False)
```

```python
import jax
import jax.numpy as jnp
from jax import lax
from jax.experimental import pallas as pl
from jax.experimental.pallas import tpu as pltpu
from jax.sharding import PartitionSpec as P


CHIPS = 8
ROWS = 4
PIECE = 64
ANY = pl.BlockSpec(memory_space=pl.ANY)
VMEM = pl.BlockSpec(memory_space=pltpu.VMEM)
SMEM = pl.BlockSpec(memory_space=pltpu.SMEM)
PARAMS = pltpu.CompilerParams(vmem_limit_bytes=12 << 20)


def ring(shift):
    return [(i, (i + shift) % ROWS) for i in range(ROWS)]


def hop(shift):
    return [(i, ((i // 2 + shift) % CHIPS) * 2 + i % 2) for i in range(2 * CHIPS)]


SWAP = [(i, i ^ 1) for i in range(2 * CHIPS)]


def both(shift):
    return [(i, ((i // 2 + (shift if i % 2 == 0 else -shift)) % CHIPS) * 2 + i % 2) for i in range(2 * CHIPS)]


def in_vmem(values):
    return [pltpu.with_memory_space_constraint(v, pltpu.VMEM) for v in values]


def call(kernel, where, vmem, rest, out, scratch, aliases=None):
    return pl.pallas_call(
        kernel,
        in_specs=[SMEM] + [VMEM] * len(vmem) + [ANY] * len(rest),
        out_specs=tuple(VMEM for _ in out),
        out_shape=tuple(pltpu.VMEM(shape, dtype) for shape, dtype in out),
        scratch_shapes=scratch,
        compiler_params=PARAMS,
        input_output_aliases={1 + i: o for i, o in (aliases or {}).items()},
    )(where, *in_vmem(vmem), *rest)


def copy_weights(where, decoders, picks, least=(0, 0)):
    _, width, count = decoders.shape
    n = len(picks)

    def kernel(where_ref, source, *refs):
        third = width // 3
        copies = [
            pltpu.make_async_copy(
                source.at[where_ref[pick], pl.ds(part * third, third)],
                refs[i].at[pl.ds(part * third, third)],
                refs[n].at[3 * i + part],
            )
            for i, pick in enumerate(picks)
            for part in range(3)
        ]
        for step in ("start", "wait"):
            for i, first in enumerate(least):

                @pl.when(where_ref[4] >= first)
                def _(i=i, step=step):
                    for copy in copies[3 * i : 3 * i + 3]:
                        getattr(copy, step)()

    out = [((width, count), decoders.dtype)] * n
    decoders = pltpu.with_memory_space_constraint(decoders, pltpu.HBM)
    return call(kernel, where, [], [decoders], out, [pltpu.SemaphoreType.DMA((3 * n,))])


def encode(where, pieces, weight, start, bias):
    half = weight.shape[0] // (2 * CHIPS)
    tokens = pieces[0][0].shape[1]
    width = weight.shape[1]
    arrays = [array for array, _ in pieces]
    halves = [place for _, places in pieces for place in places]
    vmem = [weight] + arrays + ([start] if start is not None else []) + ([bias] if bias is not None else [])

    def kernel(where_ref, weight_ref, *refs):
        pieces_refs, refs = refs[: len(arrays)], refs[len(arrays) :]
        if start is not None:
            start_ref, *refs = refs
        if bias is not None:
            bias_ref, *refs = refs
        (out_ref,) = refs
        core = where_ref[0]
        sign = 1 - 2 * core
        rows = []
        for shift, other in halves:
            at = 2 * ((where_ref[1] + sign * shift) & (CHIPS - 1)) + (1 - core if other else core)
            rows.append(weight_ref[pl.ds(pl.multiple_of(at * half, 16), half), :])
        block = jnp.concatenate([p[...] for p in pieces_refs]).T
        hidden = jnp.dot(block, jnp.concatenate(rows), preferred_element_type=jnp.float32)
        if start is not None:
            hidden = hidden + start_ref[...]
        if bias is not None:
            hidden = jnp.maximum(hidden + bias_ref[...], 0.0)
        out_ref[...] = hidden.astype(out_ref.dtype)

    out = [((tokens, width), jnp.float32 if bias is None else jnp.bfloat16)]
    return call(kernel, where, vmem, [], out, [])[0]


def gather_and_encode(where, own, weight, bias):
    other = lax.ppermute(own, "feat", SWAP)
    block = jnp.concatenate([own, other])
    b1 = lax.ppermute(block, "feat", both(1))
    b2 = lax.ppermute(block, "feat", both(2))
    b3 = lax.ppermute(b1, "feat", both(2))
    b4 = lax.ppermute(b2, "feat", both(2))
    s1 = lax.ppermute(b1, "feat", SWAP)
    s2 = lax.ppermute(b2, "feat", SWAP)
    s3 = lax.ppermute(b3, "feat", SWAP)

    def direct(piece, shift):
        return piece, [(shift, 0), (shift, 1)]

    def swapped(piece, shift):
        return piece, [(shift, 1), (shift, 0)]

    first = [direct(block, 0), direct(b1, -1), swapped(s1, 1), direct(b2, -2), swapped(s2, 2)]
    sums = encode(where, first, weight, None, None)
    return encode(where, [direct(b3, -3), swapped(s3, 3), direct(b4, -4)], weight, sums, bias)


def gather_rows(own):
    half = own.shape[0] // 2
    before = lax.ppermute(own, "row", ring(1))
    after = lax.ppermute(own, "row", ring(-1))
    before_half, after_half = before[:half], after[half:]
    first = lax.ppermute(before_half, "row", ring(1))
    second = lax.ppermute(after_half, "row", ring(-1))
    return own, before, after, first, second


def spread(where_ref, value, j, mine_ref, theirs_ref):
    core, chip, row = where_ref[0], where_ref[1], where_ref[2]
    for h in range(2):
        at = (2 * ((row + j) & (ROWS - 1)) + h - chip) & (CHIPS - 1)
        low = value[2 * h * PIECE : (2 * h + 1) * PIECE]
        high = value[(2 * h + 1) * PIECE : (2 * h + 2) * PIECE]
        mine_ref[at] = jnp.where(core == 0, low, high)
        theirs_ref[at] = jnp.where(core == 0, high, low).astype(jnp.bfloat16)


def decode_far(where, rows, turned, start, mine, theirs):
    first, second = rows

    def kernel(where_ref, first, second, turned_ref, start_ref, mine_in, theirs_in, mine_ref, theirs_ref):
        block = jnp.concatenate([first[...], second[...]])
        value = jnp.dot(block, turned_ref[...], preferred_element_type=jnp.float32) + start_ref[2]
        spread(where_ref, value, 2, mine_ref, theirs_ref)

    out = [(mine.shape, mine.dtype), (theirs.shape, theirs.dtype)]
    return call(kernel, where, [first, second, turned, start, mine, theirs], [], out, [], {4: 0, 5: 1})


def decode(where, rows, weights, start, split, only=None):
    tokens, count = rows[0].shape
    width = weights[0].shape[0]
    n = len(weights)
    m = len(rows)
    has_start = start is not None

    def kernel(where_ref, *refs):
        if only is None:
            work(where_ref, *refs)
        else:

            @pl.when(where_ref[4] == only)
            def _():
                work(where_ref, *refs)

    def work(where_ref, *refs):
        own, before, after = refs[:3]
        blocks = [(0, (own,)), (1, (after,)), (3, (before,))] + ([(2, refs[3:m])] if m == 5 else [])
        weight = refs[m][...]
        for other in refs[m + 1 : m + n]:
            weight = weight + other[...]
        rest = refs[m + n :]
        if has_start:
            start_ref, *rest = rest
        if split:
            mine_ref, theirs_ref, turned = rest
        else:
            out_ref, turned = rest
        turned[...] = weight.T
        for j, parts in blocks:
            block = parts[0][...] if len(parts) == 1 else jnp.concatenate([p[...] for p in parts])
            value = jnp.dot(block, turned[...], preferred_element_type=jnp.float32)
            if has_start:
                value = value + start_ref[j]
            if split:
                spread(where_ref, value, j, mine_ref, theirs_ref)
            else:
                out_ref[j] = value

    if split:
        shape = (CHIPS, PIECE, width)
        out = [(shape, jnp.float32), (shape, jnp.bfloat16)]
    else:
        out = [((ROWS, tokens, width), jnp.float32)]
    vmem = list(rows) + list(weights) + ([start] if has_start else [])
    turned = ((count, width), jnp.bfloat16)
    if m == 3:
        return call(kernel, where, vmem, [], out + [turned], [])
    return call(kernel, where, vmem, [], out, [pltpu.VMEM(*turned)])


def per_device(inputs, enc_weight, enc_bias, dec_weight, dec_bias):
    decoders = jnp.swapaxes(dec_weight[0], 1, 2)
    sec = lax.axis_index("sec")
    feat = lax.axis_index("feat")
    row = lax.axis_index("row")
    core, chip = feat & 1, feat >> 1
    where = jnp.stack([core, chip, row, jnp.where(sec == 2, 1, 0), sec, jnp.where(sec == 3, 1, 0), 2])
    where = where.astype(jnp.int32)

    lent_a, lent_b = copy_weights(where, decoders, (3, 6), (1, 3))
    lent_c = lax.ppermute(lent_a, "sec", [(1, 0)])
    lent_a = lax.ppermute(lent_a, "sec", [(2, 1), (3, 0)])
    lent_b = lax.ppermute(lent_b, "sec", [(3, 2)])

    features = gather_and_encode(where, inputs[0].T, enc_weight[0], enc_bias)

    every_own = gather_rows(features)
    brought = lax.ppermute(features, "sec", [(0, 2), (1, 3)])
    every_brought = gather_rows(brought)

    mine, theirs = decode(where, every_own, (lent_a, lent_b), None, True)
    pair = mine + lax.ppermute(theirs, "feat", SWAP).astype(jnp.float32)
    pair = pair.astype(jnp.bfloat16)
    back_a = lax.ppermute(pair, "sec", [(0, 3), (1, 2)])
    back_b = lax.ppermute(pair, "sec", [(2, 3)])
    mine, theirs = decode(where, every_own, (lent_c,), None, True, only=0)
    pair = mine + lax.ppermute(theirs, ("sec", "feat"), SWAP).astype(jnp.float32)
    back_c = lax.ppermute(pair.astype(jnp.bfloat16), "sec", [(0, 1)])

    own_weight, brought_weight = copy_weights(where, decoders, (4, 5))
    (start,) = decode(where, every_own, (own_weight,), None, False)
    mine, theirs, turned = decode(where, every_brought[:3], (brought_weight,), start, True)
    mine, theirs = decode_far(where, every_brought[3:], turned, start, mine, theirs)
    pair = mine + lax.ppermute(theirs, "feat", SWAP).astype(jnp.float32)
    for back in (back_a, back_b, back_c):
        pair = pair + back.astype(jnp.float32)
    send = pair.astype(jnp.bfloat16)
    up = lax.ppermute(jnp.stack([send[4], send[2]]), "feat", hop(1))
    down = lax.ppermute(send[6], "feat", hop(-1))
    got = [lax.ppermute(send[5], "feat", hop(-3))]
    for piece, extra, shift in ((3, up[0], 3), (1, up[1], 1), (7, down, -1)):
        merged = (pair[piece] + extra.astype(jnp.float32)).astype(jnp.bfloat16)
        got.append(lax.ppermute(merged, "feat", hop(shift)))
    total = pair[0]
    for g in got:
        total = total + g.astype(jnp.float32)
    return (total + dec_bias[0]).astype(jnp.bfloat16)[None]


def solution(mesh):
    in_specs = (
        P("sec", "row", "feat"),
        P("sec", None, "feat"),
        P("sec", "feat"),
        P("sec", None, "feat", "row"),
        P("sec", "row"),
    )
    out_specs = P("sec", "feat", "row")

    return jax.shard_map(per_device, mesh=mesh, in_specs=in_specs, out_specs=out_specs, check_vma=False)
```
